128 devices in a mesh: px: 8 (over y, core), py: 16 (over x, z).
Axes of the slice: x: 4, y: 4, z: 4, core: 2. Of those that a mesh axis runs over, the one named last changes fastest.
Arguments:
- initial_trace: float32 [80, 256, 2048], P(None, 'px', 'py'), may hold values from -6 to 6
- trace_rhs: float32 [80, 256, 2048], P(None, 'px', 'py'), may hold values from -6 to 6
- face_scale: float32 [256, 2048], P('px', 'py'), may hold values from 0.5 to 2
- block_inverse: float32 [80, 80], replicated, as said below
- coupling: float32 [4, 80, 80], replicated, may hold values from -0.078125 to 0.078125
- element_state: bfloat16 [320, 256, 2048], P(None, 'px', 'py'), may hold values from -6 to 6
- recover_self: bfloat16 [640, 320], replicated, may hold values from -0.25 to 0.25
- recover_faces: bfloat16 [5, 640, 80], replicated, may hold values from -0.3125 to 0.3125
- residual_map: bfloat16 [640, 640], replicated, may hold values from -0.25 to 0.25
- error_map: bfloat16 [640, 320], replicated, may hold values from -0.3125 to 0.3125
- raise_map: bfloat16 [640, 320], replicated, may hold values from -0.3125 to 0.3125
- raise_flag: int32 [256, 2048], P('px', 'py'), may hold values from 0 to 1, as said below
- new_owner: int32 [256, 2048], P('px', 'py'), may hold values from 0 to 127, as said below
Outputs:
- final_trace: float32 [80, 256, 2048], P(None, 'px', 'py')
- indicator: float32 [256, 2048], P('px', 'py')
- raised_state: bfloat16 [640, 262144], P(None, ('px', 'py'))
- moved_adjoint: bfloat16 [640, 262144], P(None, ('px', 'py'))
The draws below stay inside these ranges and needn't reach their ends.
Inputs may be any that keep to these rules, and one draw needn't show every extreme that they name: `block_inverse`: the inverse of the diagonal block shared by all faces. `raise_flag`: 1 marks an element raised in degree that moves to its new owner. `new_owner`: device index along px+py, px slowest; among one device's elements with raise_flag 1 at most 16 share one new owner, and in every draw one owner gets exactly 16 of them from every device.
All inputs are finite; a program needn't handle non-finite values.
Results may differ from the reference program's by a relative error of at most 0.0047.
Values may be sent and summed in bfloat16 or wider, within the bound.
A program may use at most 128 MiB of HBM per device.

```python
import math
import jax
import jax.numpy as jnp
from jax import lax

NB = 80
NE = 320
NE_HI = 640
CX = 32
CY = 128
SWEEPS = 2
CAP = 16
NX = 256
NY = 2048
N_PX = 8
N_PY = 16


def owner_rank_drawn(owners, flags, groups):
    members = owners.shape[0]
    position = jnp.arange(members, dtype=jnp.int32)
    sort_keys = (jnp.where(flags > 0, owners, groups) * members + position).astype(jnp.int32)
    ordering = jnp.argsort(sort_keys).astype(jnp.int32)
    group_of = (jnp.sort(sort_keys) // members).astype(jnp.int32)
    group_start = jnp.searchsorted(group_of, group_of, side='left').astype(jnp.int32)
    return jnp.zeros((members,), jnp.int32).at[ordering].set(position - group_start)


def migration_plan(key):
    base_key = jax.random.fold_in(key, 31)
    subkeys = jax.random.split(base_key, 5)
    rows_blocks = NX // CX
    cols_blocks = NY // CY
    groups = rows_blocks * cols_blocks
    members = CX * CY
    hot_owner = jax.random.randint(subkeys[0], (), 0, groups, dtype=jnp.int32)
    choose_hot = jax.random.randint(subkeys[1], (groups, members), 0, 4, dtype=jnp.int32)
    spread = jax.random.randint(subkeys[2], (groups, members), 0, groups, dtype=jnp.int32)
    chance = jax.random.randint(subkeys[3], (groups, members), 0, 1000, dtype=jnp.int32)
    offset = jax.random.randint(subkeys[4], (groups, 1), 0, members, dtype=jnp.int32)
    position = jnp.arange(members, dtype=jnp.int32)[None, :]
    forced = (position + offset) % members < CAP
    owners = jnp.where(choose_hot == 0, hot_owner, spread)
    owners = jnp.where(forced, hot_owner, owners).astype(jnp.int32)
    raw_flag = jnp.where(forced | (chance < 130), 1, 0).astype(jnp.int32)

    def rank_block(owner_block, flag_block):
        return owner_rank_drawn(owner_block, flag_block, groups)
    position_rank = jax.vmap(rank_block)(owners, raw_flag)
    flags = jnp.where(position_rank < CAP, raw_flag, 0).astype(jnp.int32)

    def layout(values):
        shaped = values.reshape(rows_blocks, cols_blocks, CX, CY)
        return jnp.transpose(shaped, (0, 2, 1, 3)).reshape(NX, NY)
    return (layout(owners), layout(flags))


def draw_new_owner(key, part):
    owners, flags = migration_plan(key)
    return owners


def draw_raise_flag(key, part):
    owners, flags = migration_plan(key)
    return flags


def draw_block_inverse(key, part):
    identity = (jnp.arange(NB)[:, None] == jnp.arange(NB)[None, :]).astype(jnp.float32)
    noise = jax.random.normal(key, (NB, NB), jnp.float32) * (0.3 / math.sqrt(NB))
    return (identity + noise).astype(jnp.float32)


def steps_of(stream_key, extent, cuts, least, top_value):
    def one(dim, shards_of):
        heights = jax.random.uniform(jax.random.fold_in(jax.random.fold_in(stream_key, 6), dim), (shards_of,), jnp.float32, least / len(cuts), top_value / len(cuts))
        return jnp.repeat(jnp.exp(heights), extent[dim] // shards_of).reshape((-1,) + (1,) * (len(extent) - dim - 1))

    factor_of = one(*cuts[0])
    for cut in cuts[1:]:
        factor_of = factor_of * one(*cut)
    return factor_of


def gaussian(own_key, dims, width, most, cuts=(), kind=jnp.bfloat16):
    loudness = steps_of(own_key, dims, cuts, -0.22, 0.18) if cuts else 1.0
    values = jax.random.normal(own_key, dims, jnp.float32) * width * loudness
    return jnp.minimum(jnp.maximum(values, -most), most).astype(kind)


def setup_inputs(seed: int = 0) -> dict:
    key_list = jax.random.split(jax.random.key(seed), 14)
    initial_trace = gaussian(key_list[0], (NB, NX, NY), 1.0, 6.0, ((1, 8), (2, 16)), jnp.float32)
    trace_rhs = gaussian(key_list[1], (NB, NX, NY), 1.0, 6.0, ((1, 8), (2, 16)), jnp.float32)
    face_scale = jnp.clip(jnp.exp(math.log(2.0) - 1.3862944 * jax.random.uniform(key_list[2], (NX, NY), jnp.float32) ** steps_of(key_list[2], (NX, NY), ((0, 8), (1, 16)), -0.2, 0.2)), 0.5, 2.0)
    block_inverse = draw_block_inverse(jax.random.fold_in(key_list[13], 71), 0)
    coupling = gaussian(key_list[4], (4, NB, NB), (NB * 70) ** -0.5, 0.078125, (), jnp.float32)
    element_state = gaussian(key_list[5], (NE, NX, NY), 1.0, 6.0, ((1, 8), (2, 16)))
    recover_self = gaussian(key_list[6], (NE_HI, NE), (2 * NE) ** -0.5, 0.25)
    recover_faces = gaussian(key_list[7], (5, NE_HI, NB), (5 * NB) ** -0.5, 0.3125)
    residual_map = gaussian(key_list[8], (NE_HI, NE_HI), NE_HI ** -0.5, 0.25)
    error_map = gaussian(key_list[9], (NE_HI, NE), NE ** -0.5, 0.3125)
    raise_map = gaussian(key_list[10], (NE_HI, NE), NE ** -0.5, 0.3125)
    raise_flag = draw_raise_flag(jax.random.fold_in(key_list[13], 71), 0)
    new_owner = draw_new_owner(jax.random.fold_in(key_list[13], 71), 0)
    return {"initial_trace": initial_trace, "trace_rhs": trace_rhs, "face_scale": face_scale, "block_inverse": block_inverse, "coupling": coupling, "element_state": element_state, "recover_self": recover_self, "recover_faces": recover_faces, "residual_map": residual_map, "error_map": error_map, "raise_map": raise_map, "raise_flag": raise_flag, "new_owner": new_owner}


exact_mode = lax.Precision.HIGHEST


def owner_rank(owners, flags, groups):
    members = owners.shape[0]
    position = jnp.arange(members, dtype=jnp.int32)
    sort_keys = (jnp.where(flags > 0, owners, groups) * members + position).astype(jnp.int32)
    ordering = jnp.argsort(sort_keys).astype(jnp.int32)
    group_of = (jnp.sort(sort_keys) // members).astype(jnp.int32)
    group_start = jnp.searchsorted(group_of, group_of, side="left").astype(jnp.int32)
    return jnp.zeros((members,), jnp.int32).at[ordering].set(position - group_start)


def relax_faces(trace, trace_rhs, face_scale, block_inverse, coupling):
    padded = jnp.pad(trace, ((0, 0), (1, 1), (1, 1)))
    beside = [padded[:, :-2, 1:-1], padded[:, 2:, 1:-1], padded[:, 1:-1, :-2], padded[:, 1:-1, 2:]]
    summed = trace_rhs
    for direction in range(4):
        summed = summed - jnp.einsum("ab,bij->aij", coupling[direction], beside[direction], precision=exact_mode)
    return face_scale[None, :, :] * jnp.einsum("ab,bij->aij", block_inverse, summed, precision=exact_mode)


def to_blocks(values):
    depth = values.shape[0]
    shaped = values.reshape(depth, N_PX, CX, N_PY, CY)
    return jnp.transpose(shaped, (1, 3, 0, 2, 4)).reshape(N_PX * N_PY, depth, CX * CY)


def reference(initial_trace, trace_rhs, face_scale, block_inverse, coupling, element_state, recover_self, recover_faces, residual_map, error_map, raise_map, raise_flag, new_owner):
    trace = initial_trace
    for sweep_count in range(SWEEPS):
        trace = relax_faces(trace, trace_rhs, face_scale, block_inverse, coupling)
    trace_half = trace.astype(jnp.bfloat16)
    padded = jnp.pad(trace_half, ((0, 0), (1, 1), (1, 1)))
    face_maps = jnp.transpose(recover_faces, (1, 0, 2)).reshape(NE_HI, 5 * NB)

    def row_block(row_index):
        row_start = (row_index * CX).astype(jnp.int32)
        window = lax.dynamic_slice_in_dim(padded, row_start, CX + 2, 1)
        own_state = lax.dynamic_slice_in_dim(element_state, row_start, CX, 1)
        face_values = jnp.concatenate([window[:, 1:-1, 1:-1], window[:, :-2, 1:-1], window[:, 2:, 1:-1], window[:, 1:-1, :-2], window[:, 1:-1, 2:]], axis=0)
        flat_state = own_state.reshape(NE, CX * NY)
        recovered = jnp.dot(recover_self, flat_state, preferred_element_type=jnp.float32) + jnp.dot(face_maps, face_values.reshape(5 * NB, CX * NY), preferred_element_type=jnp.float32)
        adjoint = recovered.astype(jnp.bfloat16)
        weighted = jnp.dot(residual_map, adjoint, preferred_element_type=jnp.float32)
        residual = jnp.dot(error_map, flat_state, preferred_element_type=jnp.float32)
        measure = jnp.mean(jnp.abs(weighted * residual), axis=0).reshape(CX, NY)
        return adjoint.reshape(NE_HI, CX, NY), measure

    adjoint_blocks, measure_blocks = lax.map(row_block, jnp.arange(N_PX, dtype=jnp.int32))
    adjoint_rec = jnp.transpose(adjoint_blocks, (1, 0, 2, 3)).reshape(NE_HI, NX, NY)
    indicator = measure_blocks.reshape(NX, NY)
    device_count = N_PX * N_PY
    owners = to_blocks(new_owner[None])[:, 0]
    flags = to_blocks(raise_flag[None])[:, 0]

    def pack_sends(state_block, adjoint_block, owner_block, flag_block):
        position_rank = owner_rank(owner_block, flag_block, device_count)
        slot_index = jnp.where(flag_block > 0, owner_block * CAP + position_rank, device_count * CAP).astype(jnp.int32)
        zero_state = jnp.zeros((NE, device_count * CAP), jnp.bfloat16)
        zero_adjoint = jnp.zeros((NE_HI, device_count * CAP), jnp.bfloat16)
        return zero_state.at[:, slot_index].set(state_block, mode="drop"), zero_adjoint.at[:, slot_index].set(adjoint_block, mode="drop")

    sent_state, sent_adjoint = jax.vmap(pack_sends)(to_blocks(element_state), to_blocks(adjoint_rec), owners, flags)

    def arrange(sent):
        depth = sent.shape[1]
        shaped = sent.reshape(device_count, depth, device_count, CAP)
        return jnp.transpose(shaped, (1, 2, 0, 3)).reshape(depth, device_count * device_count * CAP)

    moved_state = arrange(sent_state)
    moved_adjoint = arrange(sent_adjoint)
    raised_state = jnp.dot(raise_map, moved_state, preferred_element_type=jnp.float32).astype(jnp.bfloat16)
    return trace, indicator, raised_state, moved_adjoint
```

```python
import functools

import jax
import jax.numpy as jnp
from jax import lax
from jax.experimental import pallas as pl
from jax.experimental.pallas import tpu as pltpu
from jax.sharding import PartitionSpec as P

NB = 80
NE = 320
NE_HI = 640
NF = 5 * NB
ROWS = 32
LANES = 128
CELLS = ROWS * LANES
CAP = 16
F32 = jnp.float32
BF16 = jnp.bfloat16
MESH = pl.DeviceIdType.MESH
NT = (((1,), (1,)), ((), ()))


def dot(a, b):
    return jnp.dot(a, b, preferred_element_type=F32)


def dot_nt(a, b):
    return lax.dot_general(a, b, NT, preferred_element_type=F32)


def block(i):
    return pl.ds(pl.multiple_of(i * LANES, LANES), LANES)


def pack_slots(slot_ref, picker, source_ref, out_ref, chunk):
    rows_iota = lax.broadcasted_iota(jnp.int32, (chunk, LANES), 0)

    def one_chunk(m, carry):
        for i in range(ROWS):
            row = slot_ref[pl.ds(i, 1), :] - m * chunk
            picker[:, i * LANES : (i + 1) * LANES] = jnp.where(row == rows_iota, 1.0, 0.0).astype(BF16)
        found = dot_nt(picker[...], source_ref[...])
        out_ref[pl.ds(pl.multiple_of(m * chunk, chunk), chunk), :] = found.astype(BF16)
        return carry

    lax.fori_loop(0, out_ref.shape[0] // chunk, one_chunk, 0)


def state_kernel(chunk, state_ref, owner_ref, flag_ref, sent_ref, flat_ref, slot_ref, wide, picker):
    step = 1024

    def widen(c, carry):
        at = pl.ds(pl.multiple_of(c * step, step), step)
        wide[at, :] = state_ref[at, :].astype(F32)
        return carry

    lax.fori_loop(0, NE * ROWS // step, widen, 0)
    for i in range(ROWS):
        flat_ref[:, i * LANES : (i + 1) * LANES] = wide[pl.ds(i, NE, stride=ROWS), :].astype(BF16)

    owner_iota = lax.broadcasted_iota(jnp.int32, (LANES, LANES), 0)
    first = lax.broadcasted_iota(jnp.int32, (LANES, 2 * LANES), 0)
    second = lax.broadcasted_iota(jnp.int32, (LANES, 2 * LANES), 1)
    tri = jnp.where(first < second, 1.0, 0.0).astype(BF16)
    before = jnp.zeros((LANES, LANES), F32)
    for i in range(ROWS):
        owner = owner_ref[i : i + 1, :]
        flag = flag_ref[i : i + 1, :]
        hot = jnp.where((owner == owner_iota) & (flag > 0), 1.0, 0.0)
        counts = dot(hot.astype(BF16), tri)
        rank = jnp.sum(hot * (counts[:, :LANES] + before), axis=0, keepdims=True).astype(jnp.int32)
        slot_ref[i : i + 1, :] = jnp.where(flag > 0, owner * CAP + rank, -1)
        before = before + counts[:, LANES:]
    pack_slots(slot_ref, picker, flat_ref, sent_ref, chunk)


def face_kernel(chunk, slot_ref, faces_ref, sent_ref, picker):
    pack_slots(slot_ref, picker, faces_ref, sent_ref, chunk)


def sweep_kernel(
    n_px,
    n_py,
    trace_ref,
    rhs_ref,
    scale_ref,
    coupling_ref,
    inverse_ref,
    final_ref,
    faces_ref,
    coupled,
    beside,
    partial,
    edge,
    outgoing,
    halo,
    send_sem,
    recv_sem,
):
    px, py = lax.axis_index("px"), lax.axis_index("py")
    down, up = lax.rem(px + 1, n_px), lax.rem(px + n_px - 1, n_px)
    right, left = lax.rem(py + 1, n_py), lax.rem(py + n_py - 1, n_py)
    targets = ((down, py), (up, py), (px, right), (px, left))
    barrier = pltpu.get_barrier_semaphore()
    for target in targets:
        pl.semaphore_signal(barrier, inc=1, device_id=target, device_id_type=MESH)
    lane = lax.broadcasted_iota(jnp.int32, (NB, LANES), 1)

    def copies(turn):
        return [
            pltpu.make_async_remote_copy(
                src_ref=outgoing.at[turn, d],
                dst_ref=halo.at[turn, d],
                send_sem=send_sem.at[turn, d],
                recv_sem=recv_sem.at[turn, d],
                device_id=targets[d],
                device_id_type=MESH,
            )
            for d in range(4)
        ]

    present = ((px > 0), (px < n_px - 1), (py > 0), (py < n_py - 1))

    def arrived(turn, d):
        return halo[turn, d].astype(F32) * present[d].astype(jnp.int32).astype(F32)

    def emit(values, g, k, into, base, stride, turn):
        i = g * 4 + k
        half = values.astype(BF16)
        if k < 3:
            into[base : base + NB, block(i + 1)] = half
        else:

            @pl.when(g < ROWS // 4 - 1)
            def _():
                into[base : base + NB, block(i + 1)] = half

            @pl.when(g == ROWS // 4 - 1)
            def _():
                outgoing[turn, 0] = half

        if k > 0:
            into[base + stride : base + stride + NB, block(i - 1)] = half
        else:

            @pl.when(g > 0)
            def _():
                into[base + stride : base + stride + NB, block(i - 1)] = half

            @pl.when(g == 0)
            def _():
                outgoing[turn, 1] = half

        to_right = jnp.where(lane >= 1, pltpu.roll(values, 1, 1), 0.0)
        to_left = jnp.where(lane < LANES - 1, pltpu.roll(values, LANES - 1, 1), 0.0)
        into[base + 2 * stride : base + 2 * stride + NB, block(i)] = to_right.astype(BF16)
        into[base + 3 * stride : base + 3 * stride + NB, block(i)] = to_left.astype(BF16)
        edge[0] = jnp.where(lane == i, pltpu.roll(values, i + 1, 1), edge[0])
        edge[1] = jnp.where(lane == i, pltpu.roll(values, i, 1), edge[1])

    def send_all(turn):
        outgoing[turn, 2] = edge[0].astype(BF16)
        outgoing[turn, 3] = edge[1].astype(BF16)
        for copy in copies(turn):
            copy.start()

    coupled[...] = jnp.zeros_like(coupled)
    beside[...] = jnp.zeros_like(beside)
    edge[...] = jnp.zeros_like(edge)
    for d in range(4):
        coupled[:, d * LANES : d * LANES + NB] = coupling_ref[d].astype(BF16)

    def load(g, carry):
        for k in range(4):
            emit(trace_ref[pl.ds(g * 4 + k, NB, stride=ROWS), :], g, k, beside, 0, LANES, 0)
        return carry

    lax.fori_loop(0, ROWS // 4, load, 0)
    pl.semaphore_wait(barrier, 4)
    send_all(0)

    for turn in range(2):

        def before_halo(g, carry):
            wide = pl.ds(pl.multiple_of(g * 4 * LANES, 4 * LANES), 4 * LANES)
            product = dot(coupled[...], beside[:, wide])
            for k in range(4):
                i = g * 4 + k
                partial[i] = rhs_ref[pl.ds(i, NB, stride=ROWS), :] - product[:, k * LANES : (k + 1) * LANES]
            return carry

        lax.fori_loop(0, ROWS // 4, before_halo, 0)
        for copy in copies(turn):
            copy.wait()
        from_halo = [
            dot(coupled[:, d * LANES : d * LANES + NB], arrived(turn, d).astype(BF16)) for d in range(4)
        ]
        partial[0] = partial[0] - from_halo[0]
        partial[ROWS - 1] = partial[ROWS - 1] - from_halo[1]

        def after_halo(g, carry):
            sums = []
            for k in range(4):
                i = g * 4 + k
                near = jnp.where(lane == 0, pltpu.roll(from_halo[2], lax.rem(LANES - i, LANES), 1), 0.0)
                far = jnp.where(lane == LANES - 1, pltpu.roll(from_halo[3], LANES - 1 - i, 1), 0.0)
                sums.append(partial[i] - near - far)
            joined = jnp.concatenate(sums, axis=1)
            high = joined.astype(BF16)
            low = (joined - high.astype(F32)).astype(BF16)
            product = dot(inverse_ref[...], jnp.concatenate([high, low, high], axis=0))
            for k in range(4):
                i = g * 4 + k
                values = product[:, k * LANES : (k + 1) * LANES] * scale_ref[pl.ds(i, 1), :]
                if turn == 0:
                    emit(values, g, k, beside, 0, LANES, 1)
                else:
                    final_ref[pl.ds(i, NB, stride=ROWS), :] = values
                    faces_ref[:NB, block(i)] = values.astype(BF16)
                    emit(values, g, k, faces_ref, NB, NB, 2)
            return carry

        lax.fori_loop(0, ROWS // 4, after_halo, 0)
        send_all(turn + 1)

    for copy in copies(2):
        copy.wait()
    faces_ref[NB : 2 * NB, :LANES] = arrived(2, 0).astype(BF16)
    faces_ref[2 * NB : 3 * NB, CELLS - LANES :] = arrived(2, 1).astype(BF16)
    from_left = arrived(2, 2)
    from_right = arrived(2, 3)

    def mend(g, carry):
        for k in range(4):
            i = g * 4 + k
            near = pltpu.roll(from_left, lax.rem(LANES - i, LANES), 1)
            far = pltpu.roll(from_right, LANES - 1 - i, 1)
            own = faces_ref[3 * NB : 4 * NB, block(i)].astype(F32)
            faces_ref[3 * NB : 4 * NB, block(i)] = jnp.where(lane == 0, near, own).astype(BF16)
            own = faces_ref[4 * NB :, block(i)].astype(F32)
            faces_ref[4 * NB :, block(i)] = jnp.where(lane == LANES - 1, far, own).astype(BF16)
        return carry

    lax.fori_loop(0, ROWS // 4, mend, 0)


def indicator_kernel(state_ref, faces_ref, self_ref, maps_ref, residual_ref, error_ref, out_ref):
    width = 4 * LANES
    for h in range(2):
        at = slice(h * width, (h + 1) * width)
        state = state_ref[:, at]
        recovered = dot(self_ref[...], state) + dot(maps_ref[...], faces_ref[:, at])
        weighted = dot(residual_ref[...], recovered.astype(BF16))
        residual = dot(error_ref[...], state)
        means = jnp.sum(jnp.abs(weighted * residual), axis=0, keepdims=True) * (1.0 / NE_HI)
        for k in range(4):
            out_ref[h * 4 + k : h * 4 + k + 1, :] = means[:, k * LANES : (k + 1) * LANES]


def raise_kernel(moved_ref, raise_ref, out_ref):
    out_ref[...] = dot_nt(raise_ref[...], moved_ref[...]).astype(BF16)


def owner_kernel(moved_ref, faces_ref, self_ref, maps_ref, out_ref):
    recovered = dot_nt(self_ref[...], moved_ref[...]) + dot_nt(maps_ref[...], faces_ref[...])
    out_ref[...] = recovered.astype(BF16)


def whole():
    return pl.BlockSpec(memory_space=pltpu.VMEM)


def fixed(shape):
    return pl.BlockSpec(shape, lambda i: (0, 0), pipeline_mode=pl.Buffered(1))


def cost(flops, bytes_accessed):
    return pl.CostEstimate(flops=flops, bytes_accessed=bytes_accessed, transcendentals=0)


def per_device(
    n_px,
    n_py,
    initial_trace,
    trace_rhs,
    face_scale,
    block_inverse,
    coupling,
    element_state,
    recover_self,
    recover_faces,
    residual_map,
    error_map,
    raise_map,
    raise_flag,
    new_owner,
):
    slots = n_px * n_py * CAP
    chunk = 512
    sent_state, flat_state, slot_index = pl.pallas_call(
        functools.partial(state_kernel, chunk),
        out_shape=(
            jax.ShapeDtypeStruct((slots, NE), BF16),
            jax.ShapeDtypeStruct((NE, CELLS), BF16),
            jax.ShapeDtypeStruct((ROWS, LANES), jnp.int32),
        ),
        in_specs=[whole()] * 3,
        out_specs=(whole(),) * 3,
        scratch_shapes=[pltpu.VMEM((NE * ROWS, LANES), F32), pltpu.VMEM((chunk, CELLS), BF16)],
        cost_estimate=cost(2 * slots * CELLS * NE, 8 << 20),
        name="state_pack",
    )(element_state.reshape(NE * ROWS, LANES), new_owner, raise_flag)
    moved_state = lax.all_to_all(sent_state, ("px", "py"), split_axis=0, concat_axis=0, tiled=True)

    inverse_high = block_inverse.astype(BF16)
    inverse_low = (block_inverse - inverse_high.astype(F32)).astype(BF16)
    inverse_split = jnp.concatenate([inverse_high, inverse_high, inverse_low], axis=1)
    final_trace, faces = pl.pallas_call(
        functools.partial(sweep_kernel, n_px, n_py),
        out_shape=(
            jax.ShapeDtypeStruct((NB * ROWS, LANES), F32),
            jax.ShapeDtypeStruct((NF, CELLS), BF16),
        ),
        in_specs=[whole()] * 5,
        out_specs=(whole(),) * 2,
        scratch_shapes=[
            pltpu.VMEM((NB, 4 * LANES), BF16),
            pltpu.VMEM((4 * LANES, CELLS), BF16),
            pltpu.VMEM((ROWS, NB, LANES), F32),
            pltpu.VMEM((2, NB, LANES), F32),
            pltpu.VMEM((3, 4, NB, LANES), BF16),
            pltpu.VMEM((3, 4, NB, LANES), BF16),
            pltpu.SemaphoreType.DMA((3, 4)),
            pltpu.SemaphoreType.DMA((3, 4)),
        ],
        compiler_params=pltpu.CompilerParams(collective_id=0, has_side_effects=True),
        cost_estimate=cost(15 << 30, 8 << 20),
        name="sweeps",
    )(
        initial_trace.reshape(NB * ROWS, LANES),
        trace_rhs.reshape(NB * ROWS, LANES),
        face_scale,
        coupling,
        inverse_split,
    )

    sent_faces = pl.pallas_call(
        functools.partial(face_kernel, chunk),
        out_shape=jax.ShapeDtypeStruct((slots, NF), BF16),
        in_specs=[whole()] * 2,
        out_specs=whole(),
        scratch_shapes=[pltpu.VMEM((chunk, CELLS), BF16)],
        cost_estimate=cost(2 * slots * CELLS * NF, 8 << 20),
        name="face_pack",
    )(slot_index, faces)
    moved_faces = lax.all_to_all(sent_faces, ("px", "py"), split_axis=0, concat_axis=0, tiled=True)

    face_maps = jnp.transpose(recover_faces, (1, 0, 2)).reshape(NE_HI, NF)
    width = 8 * LANES
    indicator = pl.pallas_call(
        indicator_kernel,
        out_shape=jax.ShapeDtypeStruct((ROWS, LANES), F32),
        grid=(CELLS // width,),
        in_specs=[
            pl.BlockSpec((NE, width), lambda i: (0, i)),
            pl.BlockSpec((NF, width), lambda i: (0, i)),
            fixed((NE_HI, NE)),
            fixed((NE_HI, NF)),
            fixed((NE_HI, NE_HI)),
            fixed((NE_HI, NE)),
        ],
        out_specs=pl.BlockSpec((8, LANES), lambda i: (i, 0)),
        cost_estimate=cost(2 * CELLS * NE_HI * (NE + NF + NE_HI + NE), 8 << 20),
        name="recover_indicator",
    )(flat_state, faces, recover_self, face_maps, residual_map, error_map)

    part = 512
    raised_state = pl.pallas_call(
        raise_kernel,
        out_shape=jax.ShapeDtypeStruct((NE_HI, slots), BF16),
        grid=(slots // part,),
        in_specs=[pl.BlockSpec((part, NE), lambda i: (i, 0)), fixed((NE_HI, NE))],
        out_specs=pl.BlockSpec((NE_HI, part), lambda i: (0, i)),
        cost_estimate=cost(2 * slots * NE_HI * NE, 5 << 20),
        name="owner_raise",
    )(moved_state, raise_map)
    moved_adjoint = pl.pallas_call(
        owner_kernel,
        out_shape=jax.ShapeDtypeStruct((NE_HI, slots), BF16),
        grid=(slots // part,),
        in_specs=[
            pl.BlockSpec((part, NE), lambda i: (i, 0)),
            pl.BlockSpec((part, NF), lambda i: (i, 0)),
            fixed((NE_HI, NE)),
            fixed((NE_HI, NF)),
        ],
        out_specs=pl.BlockSpec((NE_HI, part), lambda i: (0, i)),
        cost_estimate=cost(2 * slots * NE_HI * (NE + NF), 6 << 20),
        name="owner_recover",
    )(moved_state, moved_faces, recover_self, face_maps)
    return (final_trace.reshape(NB, ROWS, LANES), indicator, raised_state, moved_adjoint)


def solution(mesh):
    tiles = P(None, "px", "py")
    grid = P("px", "py")
    in_specs = (tiles, tiles, grid, P(), P(), tiles, P(), P(), P(), P(), P(), grid, grid)
    out_specs = (tiles, grid, P(None, ("px", "py")), P(None, ("px", "py")))
    return jax.shard_map(
        functools.partial(per_device, mesh.shape["px"], mesh.shape["py"]),
        mesh=mesh,
        in_specs=in_specs,
        out_specs=out_specs,
        check_vma=False,
    )
```

```python
import functools

import jax
import jax.numpy as jnp
from jax import lax
from jax.experimental import pallas as pl
from jax.experimental.pallas import tpu as pltpu
from jax.sharding import PartitionSpec as P

NB = 80
NE = 320
NE_HI = 640
NF = 5 * NB
EARLY = 256
REST = NE - EARLY
LATE = 512
GROUP = 512
ROWS = 32
LANES = 128
CELLS = ROWS * LANES
CAP = 16
F32 = jnp.float32
BF16 = jnp.bfloat16
MESH = pl.DeviceIdType.MESH
NT = (((1,), (1,)), ((), ()))


def dot(a, b):
    return jnp.dot(a, b, preferred_element_type=F32)


def dot_nt(a, b):
    return lax.dot_general(a, b, NT, preferred_element_type=F32)


def block(i):
    return pl.ds(pl.multiple_of(i * LANES, LANES), LANES)


def turned(matrix, count):
    eye_row = lax.broadcasted_iota(jnp.int32, (LANES, LANES), 0)
    eye_col = lax.broadcasted_iota(jnp.int32, (LANES, LANES), 1)
    eye = jnp.where(eye_row == eye_col, 1.0, 0.0).astype(BF16)
    parts = [dot_nt(eye, matrix[:, c * LANES : (c + 1) * LANES]) for c in range(count // LANES)]
    return jnp.concatenate(parts, axis=0).astype(BF16)


def main_kernel(
    n_px,
    n_py,
    state_ref,
    owner_ref,
    flag_ref,
    trace_ref,
    rhs_ref,
    scale_ref,
    coupling_ref,
    inverse_ref,
    self_ref,
    maps_ref,
    residual_ref,
    error_ref,
    raise_ref,
    final_ref,
    indicator_ref,
    moved_early,
    moved_late,
    weights_ref,
    wide,
    early,
    late,
    slots,
    picker,
    sent_early,
    sent_late,
    late_maps,
    coupled,
    beside,
    partial,
    outgoing,
    halo,
    send_sem,
    recv_sem,
    early_send,
    early_recv,
    late_send,
    late_recv,
    self_sem,
):
    px, py = lax.axis_index("px"), lax.axis_index("py")
    devices = n_px * n_py
    me = px * n_py + py
    down, up = lax.rem(px + 1, n_px), lax.rem(px + n_px - 1, n_px)
    right, left = lax.rem(py + 1, n_py), lax.rem(py + n_py - 1, n_py)
    targets = ((down, py), (up, py), (px, right), (px, left))
    barrier = pltpu.get_barrier_semaphore()

    def place(device):
        return (lax.div(device, n_py), lax.rem(device, n_py))

    def greet(k, carry):
        pl.semaphore_signal(
            barrier, inc=1, device_id=place(lax.rem(me + k, devices)), device_id_type=MESH
        )
        return carry

    lax.fori_loop(1, devices, greet, 0)
    lane = lax.broadcasted_iota(jnp.int32, (NB, LANES), 1)

    def copies(turn):
        return [
            pltpu.make_async_remote_copy(
                src_ref=outgoing.at[turn, d],
                dst_ref=halo.at[turn, d],
                send_sem=send_sem.at[turn, d],
                recv_sem=recv_sem.at[turn, d],
                device_id=targets[d],
                device_id_type=MESH,
            )
            for d in range(4)
        ]

    present = ((px > 0), (px < n_px - 1), (py > 0), (py < n_py - 1))

    def arrived(turn, d):
        return halo[turn, d].astype(F32) * present[d].astype(jnp.int32).astype(F32)

    def emit(values, i, into, base, stride, turn, edges):
        half = values.astype(BF16)
        if i < ROWS - 1:
            into[base : base + NB, (i + 1) * LANES : (i + 2) * LANES] = half
        else:
            outgoing[turn, 0] = half
        if i > 0:
            into[base + stride : base + stride + NB, (i - 1) * LANES : i * LANES] = half
        else:
            outgoing[turn, 1] = half
        at = slice(i * LANES, (i + 1) * LANES)
        to_right = pltpu.roll(values, 1, 1)
        to_left = pltpu.roll(values, LANES - 1, 1)
        into[base + 2 * stride : base + 2 * stride + NB, at] = jnp.where(lane >= 1, to_right, 0.0).astype(BF16)
        into[base + 3 * stride : base + 3 * stride + NB, at] = jnp.where(
            lane < LANES - 1, to_left, 0.0
        ).astype(BF16)
        last = pltpu.roll(values, i + 1, 1)
        first = pltpu.roll(values, i, 1) if i else values
        return jnp.where(lane == i, last, edges[0]), jnp.where(lane == i, first, edges[1])

    def send_all(turn, edges):
        outgoing[turn, 2] = edges[0].astype(BF16)
        outgoing[turn, 3] = edges[1].astype(BF16)
        for copy in copies(turn):
            copy.start()

    no_edges = (jnp.zeros((NB, LANES), F32),) * 2

    def send_blocks(source, target_ref, sent_sem, got_sem):
        def one(k, carry):
            to = lax.rem(me + k, devices)
            pltpu.make_async_remote_copy(
                src_ref=source.at[to],
                dst_ref=target_ref.at[me],
                send_sem=sent_sem,
                recv_sem=got_sem,
                device_id=place(to),
                device_id_type=MESH,
            ).start()
            return carry

        lax.fori_loop(1, devices, one, 0)

    def wait_blocks(source, target_ref, sent_sem, got_sem):
        all_but_one = pl.ds(0, devices - 1)
        everything = pltpu.make_async_remote_copy(
            src_ref=source.at[all_but_one],
            dst_ref=target_ref.at[all_but_one],
            send_sem=sent_sem,
            recv_sem=got_sem,
            device_id=targets[0],
            device_id_type=MESH,
        )
        everything.wait_recv()
        everything.wait_send()

    def pack(source, out, first, last):
        def one(m, carry):
            at = pl.ds(pl.multiple_of(m * GROUP, GROUP), GROUP)
            found = dot_nt(picker[at, :], source[...]).astype(BF16)
            blocks = pl.ds(pl.multiple_of(m * (GROUP // CAP), GROUP // CAP), GROUP // CAP)
            out[blocks, :, :] = found.reshape(GROUP // CAP, CAP, source.shape[0])
            return carry

        lax.fori_loop(first, last, one, 0)

    def state_layout():
        step = 1024
        for c in range(NE * ROWS // step):
            at = slice(c * step, (c + 1) * step)
            wide[at, :] = state_ref[at, :].astype(F32)
        for i in range(ROWS):
            at = slice(i * LANES, (i + 1) * LANES)
            early[:, at] = wide[pl.ds(i, EARLY, stride=ROWS), :].astype(BF16)
            late[:REST, at] = wide[pl.ds(EARLY * ROWS + i, REST, stride=ROWS), :].astype(BF16)
        late[REST + NF :, :] = jnp.zeros((LATE - REST - NF, CELLS), BF16)

    def number_slots():
        owner_iota = lax.broadcasted_iota(jnp.int32, (LANES, LANES), 0)
        first = lax.broadcasted_iota(jnp.int32, (LANES, 2 * LANES), 0)
        second = lax.broadcasted_iota(jnp.int32, (LANES, 2 * LANES), 1)
        tri = jnp.where(first < second, 1.0, 0.0).astype(BF16)
        before = jnp.zeros((LANES, LANES), F32)
        for i in range(ROWS):
            owner = owner_ref[i : i + 1, :]
            flag = flag_ref[i : i + 1, :]
            hot = jnp.where((owner == owner_iota) & (flag > 0), 1.0, 0.0)
            counts = dot(hot.astype(BF16), tri)
            rank = jnp.sum(hot * (counts[:, :LANES] + before), axis=0, keepdims=True).astype(jnp.int32)
            slots[i : i + 1, :] = jnp.where(flag > 0, owner * CAP + rank, -1)
            before = before + counts[:, LANES:]

    def build_picker():
        size = 256
        rows_iota = lax.broadcasted_iota(jnp.int32, (size, LANES), 0).astype(F32).astype(BF16)
        one, zero = jnp.ones((), BF16), jnp.zeros((), BF16)

        def fill(m, carry):
            for i in range(ROWS):
                row = slots[i : i + 1, :] - m * size
                row = jnp.where((row >= 0) & (row < size), row, -1).astype(F32).astype(BF16)
                hit = jnp.where(row == rows_iota, one, zero)
                picker[pl.ds(pl.multiple_of(m * size, size), size), i * LANES : (i + 1) * LANES] = hit
            return carry

        lax.fori_loop(0, picker.shape[0] // size, fill, 0)

    def between(turn):
        if turn == 0:
            build_picker()
            pack(early, sent_early, 0, picker.shape[0] // GROUP)
        else:
            send_blocks(sent_early, moved_early, early_send, early_recv)

    coupled[...] = jnp.zeros_like(coupled)
    for d in range(4):
        coupled[:, d * LANES : d * LANES + NB] = coupling_ref[d].astype(BF16)
        beside[d * LANES + NB : (d + 1) * LANES, :] = jnp.zeros((LANES - NB, CELLS), BF16)
    beside[:NB, :LANES] = jnp.zeros((NB, LANES), BF16)
    beside[LANES : LANES + NB, CELLS - LANES :] = jnp.zeros((NB, LANES), BF16)

    state_layout()
    number_slots()
    edges = no_edges
    for i in range(ROWS):
        edges = emit(trace_ref[pl.ds(i, NB, stride=ROWS), :], i, beside, 0, LANES, 0, edges)
    pl.semaphore_wait(barrier, devices - 1)
    send_all(0, edges)
    for turn in range(2):
        between(turn)
        for g in range(ROWS // 4):
            product = dot(coupled[...], beside[:, g * 4 * LANES : (g + 1) * 4 * LANES])
            for k in range(4):
                i = g * 4 + k
                partial[i] = rhs_ref[pl.ds(i, NB, stride=ROWS), :] - product[:, k * LANES : (k + 1) * LANES]
        for copy in copies(turn):
            copy.wait()
        from_halo = [
            dot(coupled[:, d * LANES : d * LANES + NB], arrived(turn, d).astype(BF16)) for d in range(4)
        ]
        edges = no_edges
        for g in range(ROWS // 4):
            sums = []
            for k in range(4):
                i = g * 4 + k
                near = pltpu.roll(from_halo[2], LANES - i, 1) if i else from_halo[2]
                far = pltpu.roll(from_halo[3], LANES - 1 - i, 1)
                total = partial[i] - jnp.where(lane == 0, near, 0.0) - jnp.where(lane == LANES - 1, far, 0.0)
                if i == 0:
                    total = total - from_halo[0]
                if i == ROWS - 1:
                    total = total - from_halo[1]
                sums.append(total)
            joined = jnp.concatenate(sums, axis=1)
            high = joined.astype(BF16)
            low = (joined - high.astype(F32)).astype(BF16)
            product = dot(inverse_ref[...], jnp.concatenate([high, low, high], axis=0))
            for k in range(4):
                i = g * 4 + k
                values = product[:, k * LANES : (k + 1) * LANES] * scale_ref[i : i + 1, :]
                if turn == 0:
                    edges = emit(values, i, beside, 0, LANES, 1, edges)
                else:
                    final_ref[pl.ds(i, NB, stride=ROWS), :] = values
                    late[REST : REST + NB, i * LANES : (i + 1) * LANES] = values.astype(BF16)
                    edges = emit(values, i, late, REST + NB, NB, 2, edges)
        send_all(turn + 1, edges)


    late_maps[:REST, :] = self_ref[EARLY:, :]
    late_maps[REST : REST + NF, :] = maps_ref[...]
    late_maps[REST + NF :, :] = jnp.zeros((LATE - REST - NF, NE_HI), BF16)
    no_rest = jnp.zeros((LANES - REST, NE_HI), BF16)
    weigh_early = dot_nt(residual_ref[...], self_ref[:EARLY, :]).astype(BF16)
    weigh_late = dot_nt(residual_ref[...], late_maps[...]).astype(BF16)
    error_early = turned(error_ref[:EARLY, :], NE_HI)
    error_late = turned(jnp.concatenate([error_ref[EARLY:, :], no_rest], axis=0), NE_HI)
    weights_ref[:, :EARLY] = weigh_early
    weights_ref[:, EARLY : EARLY + LATE] = weigh_late
    weights_ref[:, EARLY + LATE : 2 * EARLY + LATE] = error_early
    weights_ref[:, 2 * EARLY + LATE :] = error_late
    for copy in copies(2):
        copy.wait()
    late[REST + NB : REST + 2 * NB, :LANES] = arrived(2, 0).astype(BF16)
    late[REST + 2 * NB : REST + 3 * NB, CELLS - LANES :] = arrived(2, 1).astype(BF16)
    from_left = arrived(2, 2)
    from_right = arrived(2, 3)
    for i in range(ROWS):
        at = slice(i * LANES, (i + 1) * LANES)
        near = pltpu.roll(from_left, LANES - i, 1) if i else from_left
        far = pltpu.roll(from_right, LANES - 1 - i, 1) if i < LANES - 1 else from_right
        own = late[REST + 3 * NB : REST + 4 * NB, at].astype(F32)
        late[REST + 3 * NB : REST + 4 * NB, at] = jnp.where(lane == 0, near, own).astype(BF16)
        own = late[REST + 4 * NB : REST + 5 * NB, at].astype(F32)
        late[REST + 4 * NB : REST + 5 * NB, at] = jnp.where(lane == LANES - 1, far, own).astype(BF16)
    pack(late, sent_late, 0, picker.shape[0] // GROUP)
    send_blocks(sent_late, moved_late, late_send, late_recv)
    own_early = pltpu.make_async_copy(sent_early.at[me], moved_early.at[me], self_sem.at[0])
    own_late = pltpu.make_async_copy(sent_late.at[me], moved_late.at[me], self_sem.at[1])
    own_early.start()
    own_late.start()

    width = 4 * LANES

    def measure(h, carry):
        at = pl.ds(pl.multiple_of(h * width, width), width)
        first, second = early[:, at], late[:, at]
        weighted = dot(weights_ref[:, :EARLY], first) + dot(weights_ref[:, EARLY : EARLY + LATE], second)
        residual = dot(weights_ref[:, EARLY + LATE : 2 * EARLY + LATE], first) + dot(
            weights_ref[:, 2 * EARLY + LATE :], second[:LANES, :]
        )
        means = jnp.sum(jnp.abs(weighted * residual), axis=0, keepdims=True) * (1.0 / NE_HI)
        for k in range(4):
            indicator_ref[pl.ds(h * 4 + k, 1), :] = means[:, k * LANES : (k + 1) * LANES]
        return carry

    lax.fori_loop(0, CELLS // width, measure, 0)

    weights_ref[:, :EARLY] = turned(self_ref[:EARLY, :], NE_HI)
    weights_ref[:, EARLY : EARLY + LATE] = turned(late_maps[...], NE_HI)
    weights_ref[:, EARLY + LATE : 2 * EARLY + LATE] = turned(raise_ref[:EARLY, :], NE_HI)
    weights_ref[:, 2 * EARLY + LATE :] = turned(
        jnp.concatenate([raise_ref[EARLY:, :], no_rest], axis=0), NE_HI
    )
    own_early.wait()
    own_late.wait()
    wait_blocks(sent_early, moved_early, early_send, early_recv)
    wait_blocks(sent_late, moved_late, late_send, late_recv)


def owner_kernel(early_ref, late_ref, weights_ref, raised_ref, adjoint_ref):
    part = raised_ref.shape[1]
    early = early_ref[...].reshape(part, EARLY)
    late = late_ref[...].reshape(part, LATE)
    raised = dot_nt(weights_ref[:, EARLY + LATE : 2 * EARLY + LATE], early) + dot_nt(
        weights_ref[:, 2 * EARLY + LATE :], late[:, :LANES]
    )
    raised_ref[...] = raised.astype(BF16)
    recovered = dot_nt(weights_ref[:, :EARLY], early) + dot_nt(weights_ref[:, EARLY : EARLY + LATE], late)
    adjoint_ref[...] = recovered.astype(BF16)


def whole():
    return pl.BlockSpec(memory_space=pltpu.VMEM)


def per_device(
    n_px,
    n_py,
    initial_trace,
    trace_rhs,
    face_scale,
    block_inverse,
    coupling,
    element_state,
    recover_self,
    recover_faces,
    residual_map,
    error_map,
    raise_map,
    raise_flag,
    new_owner,
):
    devices = n_px * n_py
    slots = devices * CAP
    inverse_high = block_inverse.astype(BF16)
    inverse_low = (block_inverse - inverse_high.astype(F32)).astype(BF16)
    inverse_split = jnp.concatenate([inverse_high, inverse_high, inverse_low], axis=1)
    final_trace, indicator, moved_early, moved_late, weights = pl.pallas_call(
        functools.partial(main_kernel, n_px, n_py),
        out_shape=(
            jax.ShapeDtypeStruct((NB * ROWS, LANES), F32),
            jax.ShapeDtypeStruct((ROWS, LANES), F32),
            jax.ShapeDtypeStruct((devices, CAP, EARLY), BF16),
            jax.ShapeDtypeStruct((devices, CAP, LATE), BF16),
            jax.ShapeDtypeStruct((NE_HI, 2 * EARLY + LATE + LANES), BF16),
        ),
        in_specs=[whole()] * 13,
        out_specs=(whole(),) * 5,
        scratch_shapes=[
            pltpu.VMEM((NE * ROWS, LANES), F32),
            pltpu.VMEM((EARLY, CELLS), BF16),
            pltpu.VMEM((LATE, CELLS), BF16),
            pltpu.VMEM((ROWS, LANES), jnp.int32),
            pltpu.VMEM((slots, CELLS), BF16),
            pltpu.VMEM((devices, CAP, EARLY), BF16),
            pltpu.VMEM((devices, CAP, LATE), BF16),
            pltpu.VMEM((LATE, NE_HI), BF16),
            pltpu.VMEM((NB, 4 * LANES), BF16),
            pltpu.VMEM((4 * LANES, CELLS), BF16),
            pltpu.VMEM((ROWS, NB, LANES), F32),
            pltpu.VMEM((3, 4, NB, LANES), BF16),
            pltpu.VMEM((3, 4, NB, LANES), BF16),
            pltpu.SemaphoreType.DMA((3, 4)),
            pltpu.SemaphoreType.DMA((3, 4)),
            pltpu.SemaphoreType.DMA,
            pltpu.SemaphoreType.DMA,
            pltpu.SemaphoreType.DMA,
            pltpu.SemaphoreType.DMA,
            pltpu.SemaphoreType.DMA((2,)),
        ],
        compiler_params=pltpu.CompilerParams(
            collective_id=0, has_side_effects=True, vmem_limit_bytes=64000 * 1024
        ),
        name="main",
    )(
        element_state.reshape(NE * ROWS, LANES),
        new_owner,
        raise_flag,
        initial_trace.reshape(NB * ROWS, LANES),
        trace_rhs.reshape(NB * ROWS, LANES),
        face_scale,
        coupling,
        inverse_split,
        recover_self.T,
        jnp.transpose(recover_faces, (0, 2, 1)).reshape(NF, NE_HI),
        residual_map,
        error_map.T,
        raise_map.T,
    )

    part = 32
    raised_state, moved_adjoint = pl.pallas_call(
        owner_kernel,
        out_shape=(jax.ShapeDtypeStruct((NE_HI, slots), BF16),) * 2,
        grid=(devices // part,),
        in_specs=[
            pl.BlockSpec((part, CAP, EARLY), lambda i: (i, 0, 0)),
            pl.BlockSpec((part, CAP, LATE), lambda i: (i, 0, 0)),
            pl.BlockSpec(weights.shape, lambda i: (0, 0), pipeline_mode=pl.Buffered(1)),
        ],
        out_specs=(pl.BlockSpec((NE_HI, part * CAP), lambda i: (0, i)),) * 2,
        name="owner",
    )(moved_early, moved_late, weights)
    return (final_trace.reshape(NB, ROWS, LANES), indicator, raised_state, moved_adjoint)


def solution(mesh):
    tiles = P(None, "px", "py")
    grid = P("px", "py")
    in_specs = (tiles, tiles, grid, P(), P(), tiles, P(), P(), P(), P(), P(), grid, grid)
    out_specs = (tiles, grid, P(None, ("px", "py")), P(None, ("px", "py")))
    return jax.shard_map(
        functools.partial(per_device, mesh.shape["px"], mesh.shape["py"]),
        mesh=mesh,
        in_specs=in_specs,
        out_specs=out_specs,
        check_vma=False,
    )
```

```python
import functools

import jax
import jax.numpy as jnp
from jax import lax
from jax.experimental import pallas as pl
from jax.experimental.pallas import tpu as pltpu
from jax.sharding import PartitionSpec as P

NB = 80
NE = 320
NE_HI = 640
NF = 5 * NB
EARLY = 256
REST = NE - EARLY
LATE = 512
GROUP = 512
CLASSES = 4
ROWS = 32
LANES = 128
CELLS = ROWS * LANES
CAP = 16
F32 = jnp.float32
BF16 = jnp.bfloat16
MESH = pl.DeviceIdType.MESH
NT = (((1,), (1,)), ((), ()))


def dot(a, b):
    return jnp.dot(a, b, preferred_element_type=F32)


def dot_nt(a, b):
    return lax.dot_general(a, b, NT, preferred_element_type=F32)


def block(i):
    return pl.ds(pl.multiple_of(i * LANES, LANES), LANES)


def turned(matrix, count):
    eye_row = lax.broadcasted_iota(jnp.int32, (LANES, LANES), 0)
    eye_col = lax.broadcasted_iota(jnp.int32, (LANES, LANES), 1)
    eye = jnp.where(eye_row == eye_col, 1.0, 0.0).astype(BF16)
    parts = [dot_nt(eye, matrix[:, c * LANES : (c + 1) * LANES]) for c in range(count // LANES)]
    return jnp.concatenate(parts, axis=0).astype(BF16)


def main_kernel(
    n_px,
    n_py,
    state_ref,
    owner_ref,
    flag_ref,
    trace_ref,
    rhs_ref,
    scale_ref,
    coupling_ref,
    inverse_ref,
    self_ref,
    maps_ref,
    residual_ref,
    error_ref,
    raise_ref,
    final_ref,
    indicator_ref,
    moved_early,
    moved_late,
    weights_ref,
    wide,
    early,
    late,
    slots,
    picker,
    sent_early,
    sent_late,
    late_maps,
    coupled,
    beside,
    split,
    partial,
    outgoing,
    halo,
    send_sem,
    recv_sem,
    early_send,
    early_recv,
    late_send,
    late_recv,
    self_sem,
):
    px, py = lax.axis_index("px"), lax.axis_index("py")
    devices = n_px * n_py
    me = px * n_py + py
    down, up = lax.rem(px + 1, n_px), lax.rem(px + n_px - 1, n_px)
    right, left = lax.rem(py + 1, n_py), lax.rem(py + n_py - 1, n_py)
    targets = ((down, py), (up, py), (px, right), (px, left))
    barrier = pltpu.get_barrier_semaphore()

    def place(device):
        return (lax.div(device, n_py), lax.rem(device, n_py))

    def greet(k, carry):
        pl.semaphore_signal(
            barrier, inc=1, device_id=place(lax.rem(me + k, devices)), device_id_type=MESH
        )
        return carry

    lax.fori_loop(1, devices, greet, 0)
    lane = lax.broadcasted_iota(jnp.int32, (NB, LANES), 1)

    def copies(turn):
        return [
            pltpu.make_async_remote_copy(
                src_ref=outgoing.at[turn, d],
                dst_ref=halo.at[turn, d],
                send_sem=send_sem.at[turn, d],
                recv_sem=recv_sem.at[turn, d],
                device_id=targets[d],
                device_id_type=MESH,
            )
            for d in range(4)
        ]

    present = ((px > 0), (px < n_px - 1), (py > 0), (py < n_py - 1))

    def arrived(turn, d):
        return halo[turn, d].astype(F32) * present[d].astype(jnp.int32).astype(F32)

    def emit(values, i, into, base, stride, turn, edges):
        half = values.astype(BF16)
        if i < ROWS - 1:
            into[base : base + NB, (i + 1) * LANES : (i + 2) * LANES] = half
        else:
            outgoing[turn, 0] = half
        if i > 0:
            into[base + stride : base + stride + NB, (i - 1) * LANES : i * LANES] = half
        else:
            outgoing[turn, 1] = half
        at = slice(i * LANES, (i + 1) * LANES)
        to_right = pltpu.roll(values, 1, 1)
        to_left = pltpu.roll(values, LANES - 1, 1)
        into[base + 2 * stride : base + 2 * stride + NB, at] = jnp.where(lane >= 1, to_right, 0.0).astype(BF16)
        into[base + 3 * stride : base + 3 * stride + NB, at] = jnp.where(
            lane < LANES - 1, to_left, 0.0
        ).astype(BF16)
        last = pltpu.roll(values, i + 1, 1)
        first = pltpu.roll(values, i, 1) if i else values
        return jnp.where(lane == i, last, edges[0]), jnp.where(lane == i, first, edges[1])

    def send_all(turn, edges):
        outgoing[turn, 2] = edges[0].astype(BF16)
        outgoing[turn, 3] = edges[1].astype(BF16)
        for copy in copies(turn):
            copy.start()

    no_edges = (jnp.zeros((NB, LANES), F32),) * 2

    def position(device):
        return lax.rem(device, CLASSES) * (devices // CLASSES) + lax.div(device, CLASSES)

    def send_class(shift, source, target_ref, sent_sem, got_sem):
        def one(k, carry):
            to = lax.rem(me + shift + CLASSES * k, devices)
            pltpu.make_async_remote_copy(
                src_ref=source.at[position(to)],
                dst_ref=target_ref.at[me],
                send_sem=sent_sem,
                recv_sem=got_sem,
                device_id=place(to),
                device_id_type=MESH,
            ).start()
            return carry

        lax.fori_loop(1 if shift == 0 else 0, devices // CLASSES, one, 0)

    def send_blocks(*where):
        for shift in range(CLASSES):
            send_class(shift, *where)

    def wait_blocks(source, target_ref, sent_sem, got_sem):
        all_but_one = pl.ds(0, devices - 1)
        everything = pltpu.make_async_remote_copy(
            src_ref=source.at[all_but_one],
            dst_ref=target_ref.at[all_but_one],
            send_sem=sent_sem,
            recv_sem=got_sem,
            device_id=targets[0],
            device_id_type=MESH,
        )
        everything.wait_recv()
        everything.wait_send()

    def pack(m, source, out):
        at = pl.ds(pl.multiple_of(m * GROUP, GROUP), GROUP)
        found = dot_nt(picker[at, :], source[...]).astype(BF16)
        blocks = pl.ds(pl.multiple_of(m * (GROUP // CAP), GROUP // CAP), GROUP // CAP)
        out[blocks, :, :] = found.reshape(GROUP // CAP, CAP, source.shape[0])

    def state_layout():
        step = 1024
        for c in range(NE * ROWS // step):
            at = slice(c * step, (c + 1) * step)
            wide[at, :] = state_ref[at, :].astype(F32)
        for i in range(ROWS):
            at = slice(i * LANES, (i + 1) * LANES)
            early[:, at] = wide[pl.ds(i, EARLY, stride=ROWS), :].astype(BF16)
            late[:REST, at] = wide[pl.ds(EARLY * ROWS + i, REST, stride=ROWS), :].astype(BF16)
        late[REST + NF :, :] = jnp.zeros((LATE - REST - NF, CELLS), BF16)

    def number_slots():
        owner_iota = lax.broadcasted_iota(jnp.int32, (LANES, LANES), 0)
        first = lax.broadcasted_iota(jnp.int32, (LANES, 2 * LANES), 0)
        second = lax.broadcasted_iota(jnp.int32, (LANES, 2 * LANES), 1)
        tri = jnp.where(first < second, 1.0, 0.0).astype(BF16)
        before = jnp.zeros((LANES, LANES), F32)
        for i in range(ROWS):
            owner = owner_ref[i : i + 1, :]
            flag = flag_ref[i : i + 1, :]
            hot = jnp.where((owner == owner_iota) & (flag > 0), 1.0, 0.0)
            counts = dot(hot.astype(BF16), tri)
            rank = jnp.sum(hot * (counts[:, :LANES] + before), axis=0, keepdims=True).astype(jnp.int32)
            place_of = (owner & (CLASSES - 1)) * (devices // CLASSES) + lax.shift_right_logical(owner, 2)
            slots[i : i + 1, :] = jnp.where(flag > 0, place_of * CAP + rank, -1)
            before = before + counts[:, LANES:]

    def build_picker():
        size = 256
        rows_iota = lax.broadcasted_iota(jnp.int32, (size, LANES), 0).astype(F32).astype(BF16)
        one, zero = jnp.ones((), BF16), jnp.zeros((), BF16)

        def fill(m, carry):
            for i in range(ROWS):
                row = slots[i : i + 1, :] - m * size
                row = jnp.where((row >= 0) & (row < size), row, -1).astype(F32).astype(BF16)
                hit = jnp.where(row == rows_iota, one, zero)
                picker[pl.ds(pl.multiple_of(m * size, size), size), i * LANES : (i + 1) * LANES] = hit
            return carry

        lax.fori_loop(0, picker.shape[0] // size, fill, 0)

    def between(turn):
        if turn == 0:
            build_picker()

            def one(m, carry):
                pack(m, early, sent_early)
                return carry

            lax.fori_loop(0, CLASSES, one, 0)
        else:
            send_blocks(sent_early, moved_early, early_send, early_recv)

    inverse = inverse_ref[...]
    inverse_high = inverse.astype(BF16).astype(F32)
    split[...] = jnp.concatenate([inverse_high, inverse_high, inverse - inverse_high], axis=1).astype(BF16)
    coupled[...] = jnp.zeros_like(coupled)
    for d in range(4):
        coupled[:, d * LANES : d * LANES + NB] = coupling_ref[d].astype(BF16)
        beside[d * LANES + NB : (d + 1) * LANES, :] = jnp.zeros((LANES - NB, CELLS), BF16)
    beside[:NB, :LANES] = jnp.zeros((NB, LANES), BF16)
    beside[LANES : LANES + NB, CELLS - LANES :] = jnp.zeros((NB, LANES), BF16)

    state_layout()
    number_slots()
    edges = no_edges
    for i in range(ROWS):
        edges = emit(trace_ref[pl.ds(i, NB, stride=ROWS), :], i, beside, 0, LANES, 0, edges)
    pl.semaphore_wait(barrier, devices - 1)
    send_all(0, edges)
    for turn in range(2):
        between(turn)
        for g in range(ROWS // 4):
            product = dot(coupled[...], beside[:, g * 4 * LANES : (g + 1) * 4 * LANES])
            for k in range(4):
                i = g * 4 + k
                partial[i] = rhs_ref[pl.ds(i, NB, stride=ROWS), :] - product[:, k * LANES : (k + 1) * LANES]
        for copy in copies(turn):
            copy.wait()
        from_halo = [
            dot(coupled[:, d * LANES : d * LANES + NB], arrived(turn, d).astype(BF16)) for d in range(4)
        ]
        edges = no_edges
        for g in range(ROWS // 4):
            sums = []
            for k in range(4):
                i = g * 4 + k
                near = pltpu.roll(from_halo[2], LANES - i, 1) if i else from_halo[2]
                far = pltpu.roll(from_halo[3], LANES - 1 - i, 1)
                total = partial[i] - jnp.where(lane == 0, near, 0.0) - jnp.where(lane == LANES - 1, far, 0.0)
                if i == 0:
                    total = total - from_halo[0]
                if i == ROWS - 1:
                    total = total - from_halo[1]
                sums.append(total)
            joined = jnp.concatenate(sums, axis=1)
            high = joined.astype(BF16)
            low = (joined - high.astype(F32)).astype(BF16)
            product = dot(split[...], jnp.concatenate([high, low, high], axis=0))
            for k in range(4):
                i = g * 4 + k
                values = product[:, k * LANES : (k + 1) * LANES] * scale_ref[i : i + 1, :]
                if turn == 0:
                    edges = emit(values, i, beside, 0, LANES, 1, edges)
                else:
                    final_ref[pl.ds(i, NB, stride=ROWS), :] = values
                    late[REST : REST + NB, i * LANES : (i + 1) * LANES] = values.astype(BF16)
                    edges = emit(values, i, late, REST + NB, NB, 2, edges)
        send_all(turn + 1, edges)


    late_maps[:REST, :] = self_ref[EARLY:, :]
    late_maps[REST : REST + NF, :] = maps_ref[...]
    late_maps[REST + NF :, :] = jnp.zeros((LATE - REST - NF, NE_HI), BF16)
    no_rest = jnp.zeros((LANES - REST, NE_HI), BF16)
    weigh_early = dot_nt(residual_ref[...], self_ref[:EARLY, :]).astype(BF16)
    weigh_late = dot_nt(residual_ref[...], late_maps[...]).astype(BF16)
    error_early = turned(error_ref[:EARLY, :], NE_HI)
    error_late = turned(jnp.concatenate([error_ref[EARLY:, :], no_rest], axis=0), NE_HI)
    weights_ref[:, :EARLY] = weigh_early
    weights_ref[:, EARLY : EARLY + LATE] = weigh_late
    weights_ref[:, EARLY + LATE : 2 * EARLY + LATE] = error_early
    weights_ref[:, 2 * EARLY + LATE :] = error_late
    for copy in copies(2):
        copy.wait()
    late[REST + NB : REST + 2 * NB, :LANES] = arrived(2, 0).astype(BF16)
    late[REST + 2 * NB : REST + 3 * NB, CELLS - LANES :] = arrived(2, 1).astype(BF16)
    from_left = arrived(2, 2)
    from_right = arrived(2, 3)
    for i in range(ROWS):
        at = slice(i * LANES, (i + 1) * LANES)
        near = pltpu.roll(from_left, LANES - i, 1) if i else from_left
        far = pltpu.roll(from_right, LANES - 1 - i, 1) if i < LANES - 1 else from_right
        own = late[REST + 3 * NB : REST + 4 * NB, at].astype(F32)
        late[REST + 3 * NB : REST + 4 * NB, at] = jnp.where(lane == 0, near, own).astype(BF16)
        own = late[REST + 4 * NB : REST + 5 * NB, at].astype(F32)
        late[REST + 4 * NB : REST + 5 * NB, at] = jnp.where(lane == LANES - 1, far, own).astype(BF16)
    for shift in range(CLASSES):
        pack(lax.rem(me + shift, CLASSES), late, sent_late)
        send_class(shift, sent_late, moved_late, late_send, late_recv)
    own_early = pltpu.make_async_copy(sent_early.at[position(me)], moved_early.at[me], self_sem.at[0])
    own_late = pltpu.make_async_copy(sent_late.at[position(me)], moved_late.at[me], self_sem.at[1])
    own_early.start()
    own_late.start()

    width = 4 * LANES

    def measure(h, carry):
        at = pl.ds(pl.multiple_of(h * width, width), width)
        first, second = early[:, at], late[:, at]
        weighted = dot(weights_ref[:, :EARLY], first) + dot(weights_ref[:, EARLY : EARLY + LATE], second)
        residual = dot(weights_ref[:, EARLY + LATE : 2 * EARLY + LATE], first) + dot(
            weights_ref[:, 2 * EARLY + LATE :], second[:LANES, :]
        )
        means = jnp.sum(jnp.abs(weighted * residual), axis=0, keepdims=True) * (1.0 / NE_HI)
        for k in range(4):
            indicator_ref[pl.ds(h * 4 + k, 1), :] = means[:, k * LANES : (k + 1) * LANES]
        return carry

    lax.fori_loop(0, CELLS // width, measure, 0)

    weights_ref[:, :EARLY] = turned(self_ref[:EARLY, :], NE_HI)
    weights_ref[:, EARLY : EARLY + LATE] = turned(late_maps[...], NE_HI)
    weights_ref[:, EARLY + LATE : 2 * EARLY + LATE] = turned(raise_ref[:EARLY, :], NE_HI)
    weights_ref[:, 2 * EARLY + LATE :] = turned(
        jnp.concatenate([raise_ref[EARLY:, :], no_rest], axis=0), NE_HI
    )
    own_early.wait()
    own_late.wait()
    wait_blocks(sent_early, moved_early, early_send, early_recv)
    wait_blocks(sent_late, moved_late, late_send, late_recv)


def owner_kernel(early_ref, late_ref, weights_ref, trace_ref, means_ref, raised_ref, adjoint_ref, final_ref, indicator_ref):
    final_ref[...] = trace_ref[...]
    indicator_ref[...] = means_ref[...]
    part = raised_ref.shape[1]
    early = early_ref[...].reshape(part, EARLY)
    late = late_ref[...].reshape(part, LATE)
    raised = dot_nt(weights_ref[:, EARLY + LATE : 2 * EARLY + LATE], early) + dot_nt(
        weights_ref[:, 2 * EARLY + LATE :], late[:, :LANES]
    )
    raised_ref[...] = raised.astype(BF16)
    recovered = dot_nt(weights_ref[:, :EARLY], early) + dot_nt(weights_ref[:, EARLY : EARLY + LATE], late)
    adjoint_ref[...] = recovered.astype(BF16)


def whole():
    return pl.BlockSpec(memory_space=pltpu.VMEM)


def per_device(
    n_px,
    n_py,
    initial_trace,
    trace_rhs,
    face_scale,
    block_inverse,
    coupling,
    element_state,
    recover_self,
    recover_faces,
    residual_map,
    error_map,
    raise_map,
    raise_flag,
    new_owner,
):
    devices = n_px * n_py
    slots = devices * CAP
    final_trace, indicator, moved_early, moved_late, weights = pl.pallas_call(
        functools.partial(main_kernel, n_px, n_py),
        out_shape=(
            jax.ShapeDtypeStruct((NB * ROWS, LANES), F32),
            jax.ShapeDtypeStruct((ROWS, LANES), F32),
            jax.ShapeDtypeStruct((devices, CAP, EARLY), BF16),
            jax.ShapeDtypeStruct((devices, CAP, LATE), BF16),
            jax.ShapeDtypeStruct((NE_HI, 2 * EARLY + LATE + LANES), BF16),
        ),
        in_specs=[whole()] * 13,
        out_specs=(whole(),) * 5,
        scratch_shapes=[
            pltpu.VMEM((NE * ROWS, LANES), F32),
            pltpu.VMEM((EARLY, CELLS), BF16),
            pltpu.VMEM((LATE, CELLS), BF16),
            pltpu.VMEM((ROWS, LANES), jnp.int32),
            pltpu.VMEM((slots, CELLS), BF16),
            pltpu.VMEM((devices, CAP, EARLY), BF16),
            pltpu.VMEM((devices, CAP, LATE), BF16),
            pltpu.VMEM((LATE, NE_HI), BF16),
            pltpu.VMEM((NB, 4 * LANES), BF16),
            pltpu.VMEM((4 * LANES, CELLS), BF16),
            pltpu.VMEM((NB, 3 * NB), BF16),
            pltpu.VMEM((ROWS, NB, LANES), F32),
            pltpu.VMEM((3, 4, NB, LANES), BF16),
            pltpu.VMEM((3, 4, NB, LANES), BF16),
            pltpu.SemaphoreType.DMA((3, 4)),
            pltpu.SemaphoreType.DMA((3, 4)),
            pltpu.SemaphoreType.DMA,
            pltpu.SemaphoreType.DMA,
            pltpu.SemaphoreType.DMA,
            pltpu.SemaphoreType.DMA,
            pltpu.SemaphoreType.DMA((2,)),
        ],
        compiler_params=pltpu.CompilerParams(
            collective_id=0, has_side_effects=True, vmem_limit_bytes=64000 * 1024
        ),
        name="main",
    )(
        element_state.reshape(NE * ROWS, LANES),
        new_owner,
        raise_flag,
        initial_trace.reshape(NB * ROWS, LANES),
        trace_rhs.reshape(NB * ROWS, LANES),
        face_scale,
        coupling,
        block_inverse,
        recover_self.T,
        jnp.transpose(recover_faces, (0, 2, 1)).reshape(NF, NE_HI),
        residual_map,
        error_map.T,
        raise_map.T,
    )

    part = 32
    steps = devices // part
    passed = (
        pl.BlockSpec((NB * ROWS // steps, LANES), lambda i: (i, 0)),
        pl.BlockSpec((ROWS // steps, LANES), lambda i: (i, 0)),
    )
    raised_state, moved_adjoint, final_trace, indicator = pl.pallas_call(
        owner_kernel,
        out_shape=(jax.ShapeDtypeStruct((NE_HI, slots), BF16),) * 2
        + (
            jax.ShapeDtypeStruct((NB * ROWS, LANES), F32),
            jax.ShapeDtypeStruct((ROWS, LANES), F32),
        ),
        grid=(steps,),
        in_specs=[
            pl.BlockSpec((part, CAP, EARLY), lambda i: (i, 0, 0)),
            pl.BlockSpec((part, CAP, LATE), lambda i: (i, 0, 0)),
            pl.BlockSpec(weights.shape, lambda i: (0, 0), pipeline_mode=pl.Buffered(1)),
            *passed,
        ],
        out_specs=(pl.BlockSpec((NE_HI, part * CAP), lambda i: (0, i)),) * 2 + passed,
        name="owner",
    )(moved_early, moved_late, weights, final_trace, indicator)
    return (final_trace.reshape(NB, ROWS, LANES), indicator, raised_state, moved_adjoint)


def solution(mesh):
    tiles = P(None, "px", "py")
    grid = P("px", "py")
    in_specs = (tiles, tiles, grid, P(), P(), tiles, P(), P(), P(), P(), P(), grid, grid)
    out_specs = (tiles, grid, P(None, ("px", "py")), P(None, ("px", "py")))
    return jax.shard_map(
        functools.partial(per_device, mesh.shape["px"], mesh.shape["py"]),
        mesh=mesh,
        in_specs=in_specs,
        out_specs=out_specs,
        check_vma=False,
    )
```

```python
import functools

import jax
import jax.numpy as jnp
from jax import lax
from jax.experimental import pallas as pl
from jax.experimental.pallas import tpu as pltpu
from jax.sharding import PartitionSpec as P

NB = 80
NE = 320
NE_HI = 640
NF = 5 * NB
EARLY = 256
REST = NE - EARLY
LATE = 512
GROUP = 512
CLASSES = 4
ROWS = 32
LANES = 128
CELLS = ROWS * LANES
CAP = 16
F32 = jnp.float32
BF16 = jnp.bfloat16
MESH = pl.DeviceIdType.MESH
NT = (((1,), (1,)), ((), ()))


def dot(a, b):
    return jnp.dot(a, b, preferred_element_type=F32)


def dot_nt(a, b):
    return lax.dot_general(a, b, NT, preferred_element_type=F32)


def block(i):
    return pl.ds(pl.multiple_of(i * LANES, LANES), LANES)


def turned(matrix, count):
    eye_row = lax.broadcasted_iota(jnp.int32, (LANES, LANES), 0)
    eye_col = lax.broadcasted_iota(jnp.int32, (LANES, LANES), 1)
    eye = jnp.where(eye_row == eye_col, 1.0, 0.0).astype(BF16)
    parts = [dot_nt(eye, matrix[:, c * LANES : (c + 1) * LANES]) for c in range(count // LANES)]
    return jnp.concatenate(parts, axis=0).astype(BF16)


def main_kernel(
    n_px,
    n_py,
    state_ref,
    owner_ref,
    flag_ref,
    trace_ref,
    rhs_ref,
    scale_ref,
    coupling_ref,
    inverse_ref,
    self_ref,
    maps_ref,
    residual_ref,
    error_ref,
    raise_ref,
    final_ref,
    indicator_ref,
    moved_early,
    moved_late,
    weights_ref,
    wide,
    early,
    late,
    slots,
    picker,
    sent_early,
    sent_late,
    late_maps,
    coupled,
    beside,
    split,
    partial,
    outgoing,
    halo,
    send_sem,
    recv_sem,
    early_send,
    early_recv,
    late_send,
    late_recv,
    self_sem,
):
    px, py = lax.axis_index("px"), lax.axis_index("py")
    devices = n_px * n_py
    me = px * n_py + py
    down, up = lax.rem(px + 1, n_px), lax.rem(px + n_px - 1, n_px)
    right, left = lax.rem(py + 1, n_py), lax.rem(py + n_py - 1, n_py)
    targets = ((down, py), (up, py), (px, right), (px, left))
    barrier = pltpu.get_barrier_semaphore()

    def place(device):
        return (lax.div(device, n_py), lax.rem(device, n_py))

    def greet(k, carry):
        pl.semaphore_signal(
            barrier, inc=1, device_id=place(lax.rem(me + k, devices)), device_id_type=MESH
        )
        return carry

    lax.fori_loop(1, devices, greet, 0)
    lane = lax.broadcasted_iota(jnp.int32, (NB, LANES), 1)

    def copies(turn):
        return [
            pltpu.make_async_remote_copy(
                src_ref=outgoing.at[turn, d],
                dst_ref=halo.at[turn, d],
                send_sem=send_sem.at[turn, d],
                recv_sem=recv_sem.at[turn, d],
                device_id=targets[d],
                device_id_type=MESH,
            )
            for d in range(4)
        ]

    present = ((px > 0), (px < n_px - 1), (py > 0), (py < n_py - 1))

    def arrived(turn, d):
        return halo[turn, d].astype(F32) * present[d].astype(jnp.int32).astype(F32)

    def emit(values, i, into, base, stride, turn, edges):
        half = values.astype(BF16)
        if i < ROWS - 1:
            into[base : base + NB, (i + 1) * LANES : (i + 2) * LANES] = half
        else:
            outgoing[turn, 0] = half
        if i > 0:
            into[base + stride : base + stride + NB, (i - 1) * LANES : i * LANES] = half
        else:
            outgoing[turn, 1] = half
        at = slice(i * LANES, (i + 1) * LANES)
        to_right = pltpu.roll(values, 1, 1)
        to_left = pltpu.roll(values, LANES - 1, 1)
        into[base + 2 * stride : base + 2 * stride + NB, at] = jnp.where(lane >= 1, to_right, 0.0).astype(BF16)
        into[base + 3 * stride : base + 3 * stride + NB, at] = jnp.where(
            lane < LANES - 1, to_left, 0.0
        ).astype(BF16)
        last = pltpu.roll(values, i + 1, 1)
        first = pltpu.roll(values, i, 1) if i else values
        return jnp.where(lane == i, last, edges[0]), jnp.where(lane == i, first, edges[1])

    def send_all(turn, edges):
        outgoing[turn, 2] = edges[0].astype(BF16)
        outgoing[turn, 3] = edges[1].astype(BF16)
        for copy in copies(turn):
            copy.start()

    no_edges = (jnp.zeros((NB, LANES), F32),) * 2

    def position(device):
        return lax.rem(device, CLASSES) * (devices // CLASSES) + lax.div(device, CLASSES)

    def send_class(shift, source, target_ref, sent_sem, got_sem):
        def one(k, carry):
            to = lax.rem(me + shift + CLASSES * k, devices)
            pltpu.make_async_remote_copy(
                src_ref=source.at[position(to)],
                dst_ref=target_ref.at[me],
                send_sem=sent_sem,
                recv_sem=got_sem,
                device_id=place(to),
                device_id_type=MESH,
            ).start()
            return carry

        lax.fori_loop(1 if shift == 0 else 0, devices // CLASSES, one, 0)

    def wait_blocks(source, target_ref, sent_sem, got_sem):
        all_but_one = pl.ds(0, devices - 1)
        everything = pltpu.make_async_remote_copy(
            src_ref=source.at[all_but_one],
            dst_ref=target_ref.at[all_but_one],
            send_sem=sent_sem,
            recv_sem=got_sem,
            device_id=targets[0],
            device_id_type=MESH,
        )
        everything.wait_recv()
        everything.wait_send()

    def pack(m, source, out):
        at = pl.ds(pl.multiple_of(m * GROUP, GROUP), GROUP)
        found = dot_nt(picker[at, :], source[...]).astype(BF16)
        blocks = pl.ds(pl.multiple_of(m * (GROUP // CAP), GROUP // CAP), GROUP // CAP)
        out[blocks, :, :] = found.reshape(GROUP // CAP, CAP, source.shape[0])

    def state_layout():
        step = 1024
        for c in range(NE * ROWS // step):
            at = slice(c * step, (c + 1) * step)
            wide[at, :] = state_ref[at, :].astype(F32)
        for i in range(ROWS):
            at = slice(i * LANES, (i + 1) * LANES)
            early[:, at] = wide[pl.ds(i, EARLY, stride=ROWS), :].astype(BF16)
            late[:REST, at] = wide[pl.ds(EARLY * ROWS + i, REST, stride=ROWS), :].astype(BF16)
        late[REST + NF :, :] = jnp.zeros((LATE - REST - NF, CELLS), BF16)

    def number_slots():
        owner_iota = lax.broadcasted_iota(jnp.int32, (LANES, LANES), 0)
        first = lax.broadcasted_iota(jnp.int32, (LANES, 2 * LANES), 0)
        second = lax.broadcasted_iota(jnp.int32, (LANES, 2 * LANES), 1)
        tri = jnp.where(first < second, 1.0, 0.0).astype(BF16)
        before = jnp.zeros((LANES, LANES), F32)
        for i in range(ROWS):
            owner = owner_ref[i : i + 1, :]
            flag = flag_ref[i : i + 1, :]
            hot = jnp.where((owner == owner_iota) & (flag > 0), 1.0, 0.0)
            counts = dot(hot.astype(BF16), tri)
            rank = jnp.sum(hot * (counts[:, :LANES] + before), axis=0, keepdims=True).astype(jnp.int32)
            place_of = (owner & (CLASSES - 1)) * (devices // CLASSES) + lax.shift_right_logical(owner, 2)
            slots[i : i + 1, :] = jnp.where(flag > 0, place_of * CAP + rank, -1)
            before = before + counts[:, LANES:]

    def build_picker():
        size = 256
        rows_iota = lax.broadcasted_iota(jnp.int32, (size, LANES), 0).astype(F32).astype(BF16)
        one, zero = jnp.ones((), BF16), jnp.zeros((), BF16)

        def fill(m, carry):
            for i in range(ROWS):
                row = slots[i : i + 1, :] - m * size
                row = jnp.where((row >= 0) & (row < size), row, -1).astype(F32).astype(BF16)
                hit = jnp.where(row == rows_iota, one, zero)
                picker[pl.ds(pl.multiple_of(m * size, size), size), i * LANES : (i + 1) * LANES] = hit
            return carry

        lax.fori_loop(0, picker.shape[0] // size, fill, 0)

    def between(turn):
        if turn == 0:
            build_picker()
            for shift in range(CLASSES):
                pack(lax.rem(me + shift, CLASSES), early, sent_early)
                if shift < CLASSES // 2:
                    send_class(shift, sent_early, moved_early, early_send, early_recv)
        else:
            for shift in range(CLASSES // 2, CLASSES):
                send_class(shift, sent_early, moved_early, early_send, early_recv)

    inverse = inverse_ref[...]
    inverse_high = inverse.astype(BF16).astype(F32)
    split[...] = jnp.concatenate([inverse_high, inverse_high, inverse - inverse_high], axis=1).astype(BF16)
    coupled[...] = jnp.zeros_like(coupled)
    for d in range(4):
        coupled[:, d * LANES : d * LANES + NB] = coupling_ref[d].astype(BF16)
        beside[d * LANES + NB : (d + 1) * LANES, :] = jnp.zeros((LANES - NB, CELLS), BF16)
    beside[:NB, :LANES] = jnp.zeros((NB, LANES), BF16)
    beside[LANES : LANES + NB, CELLS - LANES :] = jnp.zeros((NB, LANES), BF16)

    state_layout()
    number_slots()
    edges = no_edges
    for i in range(ROWS):
        edges = emit(trace_ref[pl.ds(i, NB, stride=ROWS), :], i, beside, 0, LANES, 0, edges)
    pl.semaphore_wait(barrier, devices - 1)
    send_all(0, edges)
    for turn in range(2):
        between(turn)
        for g in range(ROWS // 4):
            product = dot(coupled[...], beside[:, g * 4 * LANES : (g + 1) * 4 * LANES])
            for k in range(4):
                i = g * 4 + k
                partial[i] = rhs_ref[pl.ds(i, NB, stride=ROWS), :] - product[:, k * LANES : (k + 1) * LANES]
        for copy in copies(turn):
            copy.wait()
        from_halo = [
            dot(coupled[:, d * LANES : d * LANES + NB], arrived(turn, d).astype(BF16)) for d in range(4)
        ]
        edges = no_edges
        for g in range(ROWS // 4):
            sums = []
            for k in range(4):
                i = g * 4 + k
                near = pltpu.roll(from_halo[2], LANES - i, 1) if i else from_halo[2]
                far = pltpu.roll(from_halo[3], LANES - 1 - i, 1)
                total = partial[i] - jnp.where(lane == 0, near, 0.0) - jnp.where(lane == LANES - 1, far, 0.0)
                if i == 0:
                    total = total - from_halo[0]
                if i == ROWS - 1:
                    total = total - from_halo[1]
                sums.append(total)
            joined = jnp.concatenate(sums, axis=1)
            high = joined.astype(BF16)
            low = (joined - high.astype(F32)).astype(BF16)
            product = dot(split[...], jnp.concatenate([high, low, high], axis=0))
            for k in range(4):
                i = g * 4 + k
                values = product[:, k * LANES : (k + 1) * LANES] * scale_ref[i : i + 1, :]
                if turn == 0:
                    edges = emit(values, i, beside, 0, LANES, 1, edges)
                else:
                    final_ref[pl.ds(i, NB, stride=ROWS), :] = values
                    late[REST : REST + NB, i * LANES : (i + 1) * LANES] = values.astype(BF16)
                    edges = emit(values, i, late, REST + NB, NB, 2, edges)
        send_all(turn + 1, edges)


    late_maps[:REST, :] = self_ref[EARLY:, :]
    late_maps[REST : REST + NF, :] = maps_ref[...]
    late_maps[REST + NF :, :] = jnp.zeros((LATE - REST - NF, NE_HI), BF16)
    no_rest = jnp.zeros((LANES - REST, NE_HI), BF16)
    weigh_early = dot_nt(residual_ref[...], self_ref[:EARLY, :]).astype(BF16)
    weigh_late = dot_nt(residual_ref[...], late_maps[...]).astype(BF16)
    error_early = turned(error_ref[:EARLY, :], NE_HI)
    error_late = turned(jnp.concatenate([error_ref[EARLY:, :], no_rest], axis=0), NE_HI)
    weights_ref[:, :EARLY] = weigh_early
    weights_ref[:, EARLY : EARLY + LATE] = weigh_late
    weights_ref[:, EARLY + LATE : 2 * EARLY + LATE] = error_early
    weights_ref[:, 2 * EARLY + LATE :] = error_late
    for copy in copies(2):
        copy.wait()
    late[REST + NB : REST + 2 * NB, :LANES] = arrived(2, 0).astype(BF16)
    late[REST + 2 * NB : REST + 3 * NB, CELLS - LANES :] = arrived(2, 1).astype(BF16)
    from_left = arrived(2, 2)
    from_right = arrived(2, 3)
    for i in range(ROWS):
        at = slice(i * LANES, (i + 1) * LANES)
        near = pltpu.roll(from_left, LANES - i, 1) if i else from_left
        far = pltpu.roll(from_right, LANES - 1 - i, 1) if i < LANES - 1 else from_right
        own = late[REST + 3 * NB : REST + 4 * NB, at].astype(F32)
        late[REST + 3 * NB : REST + 4 * NB, at] = jnp.where(lane == 0, near, own).astype(BF16)
        own = late[REST + 4 * NB : REST + 5 * NB, at].astype(F32)
        late[REST + 4 * NB : REST + 5 * NB, at] = jnp.where(lane == LANES - 1, far, own).astype(BF16)
    for shift in range(CLASSES):
        pack(lax.rem(me + shift, CLASSES), late, sent_late)
        send_class(shift, sent_late, moved_late, late_send, late_recv)
    own_early = pltpu.make_async_copy(sent_early.at[position(me)], moved_early.at[me], self_sem.at[0])
    own_late = pltpu.make_async_copy(sent_late.at[position(me)], moved_late.at[me], self_sem.at[1])
    own_early.start()
    own_late.start()

    width = 4 * LANES

    def measure(h, carry):
        at = pl.ds(pl.multiple_of(h * width, width), width)
        first, second = early[:, at], late[:, at]
        weighted = dot(weights_ref[:, :EARLY], first) + dot(weights_ref[:, EARLY : EARLY + LATE], second)
        residual = dot(weights_ref[:, EARLY + LATE : 2 * EARLY + LATE], first) + dot(
            weights_ref[:, 2 * EARLY + LATE :], second[:LANES, :]
        )
        means = jnp.sum(jnp.abs(weighted * residual), axis=0, keepdims=True) * (1.0 / NE_HI)
        for k in range(4):
            indicator_ref[pl.ds(h * 4 + k, 1), :] = means[:, k * LANES : (k + 1) * LANES]
        return carry

    lax.fori_loop(0, CELLS // width, measure, 0)

    weights_ref[:, :EARLY] = turned(self_ref[:EARLY, :], NE_HI)
    weights_ref[:, EARLY : EARLY + LATE] = turned(late_maps[...], NE_HI)
    weights_ref[:, EARLY + LATE : 2 * EARLY + LATE] = turned(raise_ref[:EARLY, :], NE_HI)
    weights_ref[:, 2 * EARLY + LATE :] = turned(
        jnp.concatenate([raise_ref[EARLY:, :], no_rest], axis=0), NE_HI
    )
    own_early.wait()
    own_late.wait()
    wait_blocks(sent_early, moved_early, early_send, early_recv)
    wait_blocks(sent_late, moved_late, late_send, late_recv)


def owner_kernel(early_ref, late_ref, weights_ref, trace_ref, means_ref, raised_ref, adjoint_ref, final_ref, indicator_ref):
    final_ref[...] = trace_ref[...]
    indicator_ref[...] = means_ref[...]
    part = raised_ref.shape[1]
    early = early_ref[...].reshape(part, EARLY)
    late = late_ref[...].reshape(part, LATE)
    raised = dot_nt(weights_ref[:, EARLY + LATE : 2 * EARLY + LATE], early) + dot_nt(
        weights_ref[:, 2 * EARLY + LATE :], late[:, :LANES]
    )
    raised_ref[...] = raised.astype(BF16)
    recovered = dot_nt(weights_ref[:, :EARLY], early) + dot_nt(weights_ref[:, EARLY : EARLY + LATE], late)
    adjoint_ref[...] = recovered.astype(BF16)


def whole():
    return pl.BlockSpec(memory_space=pltpu.VMEM)


def per_device(
    n_px,
    n_py,
    initial_trace,
    trace_rhs,
    face_scale,
    block_inverse,
    coupling,
    element_state,
    recover_self,
    recover_faces,
    residual_map,
    error_map,
    raise_map,
    raise_flag,
    new_owner,
):
    devices = n_px * n_py
    slots = devices * CAP
    final_trace, indicator, moved_early, moved_late, weights = pl.pallas_call(
        functools.partial(main_kernel, n_px, n_py),
        out_shape=(
            jax.ShapeDtypeStruct((NB * ROWS, LANES), F32),
            jax.ShapeDtypeStruct((ROWS, LANES), F32),
            jax.ShapeDtypeStruct((devices, CAP, EARLY), BF16),
            jax.ShapeDtypeStruct((devices, CAP, LATE), BF16),
            jax.ShapeDtypeStruct((NE_HI, 2 * EARLY + LATE + LANES), BF16),
        ),
        in_specs=[whole()] * 13,
        out_specs=(whole(),) * 5,
        scratch_shapes=[
            pltpu.VMEM((NE * ROWS, LANES), F32),
            pltpu.VMEM((EARLY, CELLS), BF16),
            pltpu.VMEM((LATE, CELLS), BF16),
            pltpu.VMEM((ROWS, LANES), jnp.int32),
            pltpu.VMEM((slots, CELLS), BF16),
            pltpu.VMEM((devices, CAP, EARLY), BF16),
            pltpu.VMEM((devices, CAP, LATE), BF16),
            pltpu.VMEM((LATE, NE_HI), BF16),
            pltpu.VMEM((NB, 4 * LANES), BF16),
            pltpu.VMEM((4 * LANES, CELLS), BF16),
            pltpu.VMEM((NB, 3 * NB), BF16),
            pltpu.VMEM((ROWS, NB, LANES), F32),
            pltpu.VMEM((3, 4, NB, LANES), BF16),
            pltpu.VMEM((3, 4, NB, LANES), BF16),
            pltpu.SemaphoreType.DMA((3, 4)),
            pltpu.SemaphoreType.DMA((3, 4)),
            pltpu.SemaphoreType.DMA,
            pltpu.SemaphoreType.DMA,
            pltpu.SemaphoreType.DMA,
            pltpu.SemaphoreType.DMA,
            pltpu.SemaphoreType.DMA((2,)),
        ],
        compiler_params=pltpu.CompilerParams(
            collective_id=0, has_side_effects=True, vmem_limit_bytes=64000 * 1024
        ),
        name="main",
    )(
        element_state.reshape(NE * ROWS, LANES),
        new_owner,
        raise_flag,
        initial_trace.reshape(NB * ROWS, LANES),
        trace_rhs.reshape(NB * ROWS, LANES),
        face_scale,
        coupling,
        block_inverse,
        recover_self.T,
        jnp.transpose(recover_faces, (0, 2, 1)).reshape(NF, NE_HI),
        residual_map,
        error_map.T,
        raise_map.T,
    )

    part = 32
    steps = devices // part
    passed = (
        pl.BlockSpec((NB * ROWS // steps, LANES), lambda i: (i, 0)),
        pl.BlockSpec((ROWS // steps, LANES), lambda i: (i, 0)),
    )
    raised_state, moved_adjoint, final_trace, indicator = pl.pallas_call(
        owner_kernel,
        out_shape=(jax.ShapeDtypeStruct((NE_HI, slots), BF16),) * 2
        + (
            jax.ShapeDtypeStruct((NB * ROWS, LANES), F32),
            jax.ShapeDtypeStruct((ROWS, LANES), F32),
        ),
        grid=(steps,),
        in_specs=[
            pl.BlockSpec((part, CAP, EARLY), lambda i: (i, 0, 0)),
            pl.BlockSpec((part, CAP, LATE), lambda i: (i, 0, 0)),
            pl.BlockSpec(weights.shape, lambda i: (0, 0), pipeline_mode=pl.Buffered(1)),
            *passed,
        ],
        out_specs=(pl.BlockSpec((NE_HI, part * CAP), lambda i: (0, i)),) * 2 + passed,
        name="owner",
    )(moved_early, moved_late, weights, final_trace, indicator)
    return (final_trace.reshape(NB, ROWS, LANES), indicator, raised_state, moved_adjoint)


def solution(mesh):
    tiles = P(None, "px", "py")
    grid = P("px", "py")
    in_specs = (tiles, tiles, grid, P(), P(), tiles, P(), P(), P(), P(), P(), grid, grid)
    out_specs = (tiles, grid, P(None, ("px", "py")), P(None, ("px", "py")))
    return jax.shard_map(
        functools.partial(per_device, mesh.shape["px"], mesh.shape["py"]),
        mesh=mesh,
        in_specs=in_specs,
        out_specs=out_specs,
        check_vma=False,
    )
```
